32 devices in a mesh: row: 8 (over y, x, core), col: 4 (over z).
Axes of the slice: x: 2, y: 2, z: 4, core: 2. Of those that a mesh axis runs over, the one named last changes fastest.
Arguments:
- resident_inverse: bfloat16 [24576, 24576], P('row', 'col')
- factor: bfloat16 [3, 24576, 512], P(None, 'row', 'col'), may hold values from -0.15625 to 0.15625
- diag_inverse: float32 [3, 512, 512], P(None, None, 'col'), may hold values from -4 to 4
- anc_tiles: int32 [3, 64], replicated, may hold values from -1 to 95, as said below
- slot_tile: int32 [96], replicated, may hold values from 0 to 95, as said below
Outputs:
- new_cols: bfloat16 [3, 24576, 512], P(None, 'row', 'col')
- diag_blocks: float32 [3, 512, 512], P(None, None, 'col')
The draws below stay inside these ranges and needn't reach their ends.
Inputs may be any that keep to these rules, and one draw needn't show every extreme that they name: `anc_tiles`: row j lists the ancestor tiles of supernode j in ascending order, each at most once, followed by -1 in unused entries; every list holds tile 96 - 1; list 0 is full and list 2 has fewer than 32 tiles. A permutation of the tiles; slot s holds tile slot_tile[s], and each tile is stored within the same block of 24 consecutive slots as its own index. `resident_inverse` is symmetric. `resident_inverse` is symmetric.
All inputs are finite; a program needn't handle non-finite values.
Results may differ from the reference program's by a relative error of at most 0.017.
Values may be sent and summed in bfloat16 or wider, within the bound.
A program may use at most 128 MiB of HBM per device.

```python
import jax
import jax.numpy as jnp
from jax import lax

NA = 24576
W = 512
TB = 256
SUPERS = 3
MAXT = 64
NT = 96
OWN_TILES = 24
N_ROW = 8
N_COL = 4


def draw_resident_inverse(key, part):
    key_main = jax.random.fold_in(key, 101)
    spread = 1.5 / NA ** 0.5
    noise = jax.random.normal(key_main, (NA, NA), jnp.float32)
    sym = (noise + noise.T) * (0.70710678 * spread)
    sym = sym + jnp.eye(NA, dtype=jnp.float32)
    return sym.astype(jnp.bfloat16)


def draw_anc_tiles(key, part):
    tile_ids = jnp.arange(NT, dtype=jnp.int32)
    key_pick = jax.random.fold_in(key, 303)
    count_one = jax.random.randint(jax.random.fold_in(key, 404), (), MAXT // 2, MAXT)
    count_two = jax.random.randint(jax.random.fold_in(key, 505), (), MAXT // 4, MAXT // 2)
    counts = jnp.stack([jnp.int32(MAXT), count_one.astype(jnp.int32), count_two.astype(jnp.int32)])
    listing = []
    for which in range(SUPERS):
        raw_scores = jax.random.randint(jax.random.fold_in(key_pick, which), (NT,), 0, NT)
        scores = (raw_scores + tile_ids) * NT + tile_ids
        scores = jnp.where(tile_ids == NT - 1, 4 * NT * NT, scores)
        ranking = jnp.argsort(-scores, stable=True).astype(jnp.int32)
        chosen = ranking[:MAXT]
        in_list = jnp.arange(MAXT, dtype=jnp.int32) < counts[which % 3]
        chosen = jnp.where(in_list, chosen, NT + 1)
        chosen = jnp.sort(chosen)
        listing.append(jnp.where(chosen > NT - 1, -1, chosen).astype(jnp.int32))
    return jnp.stack(listing)


def draw_slot_tile(key, part):
    tile_ids = jnp.arange(NT, dtype=jnp.int32)
    raw_scores = jax.random.randint(jax.random.fold_in(key, 606), (NT,), 0, NT)
    groups = tile_ids // OWN_TILES
    scores = groups * (NT * NT) + raw_scores * NT + tile_ids
    return jnp.argsort(scores, stable=True).astype(jnp.int32)


def strengthened(drawn, rng, source, target, blocks, factor):
    def block_of(position):
        return (jnp.arange(drawn.shape[position]) // (drawn.shape[position] // blocks)).reshape((-1,) + (1,) * (drawn.ndim - 1 - position))

    first = jax.random.permutation(rng, blocks)[block_of(target)]
    far = (block_of(target) + blocks // 2) % blocks
    return jnp.where((block_of(source) == first) | (block_of(source) == far), factor * drawn, drawn)


def steps_of(own_key, extent, pieces, smallest, largest):
    gain = 1.0
    for axis_at, parts in pieces:
        draws = jax.random.uniform(jax.random.fold_in(jax.random.fold_in(own_key, 6), axis_at), (parts,), jnp.float32, smallest / len(pieces), largest / len(pieces))
        gain = gain * jnp.repeat(jnp.exp(draws), extent[axis_at] // parts).reshape((-1,) + (1,) * (len(extent) - 1 - axis_at))
    return gain


def gaussian(key, extent, deviation, limit, shards=(), kind=jnp.bfloat16):
    drawn = deviation * jax.random.normal(key, extent, jnp.float32)
    if shards:
        drawn = drawn * steps_of(key, extent, shards, -0.22, 0.18)
    return jnp.clip(drawn, -limit, limit).astype(kind)


def bell_draw_with(own_key, dims, scale, most, split, heavy, held_as=jnp.bfloat16):
    array = scale * jax.random.normal(own_key, dims, jnp.float32)
    if split:
        array = array * steps_of(own_key, dims, split, -0.22, 0.18)
    return jnp.clip(strengthened(array, jax.random.fold_in(own_key, 3), *heavy), -most, most).astype(held_as)


def setup_inputs(seed: int = 0) -> dict:
    seeds = jax.random.split(jax.random.key(seed), 6)
    resident_inverse = draw_resident_inverse(jax.random.fold_in(seeds[5], 71), 0)
    factor = bell_draw_with(seeds[1], (SUPERS, NA, W), (NA // N_ROW) ** -0.5, 0.15625, ((1, 8), (2, 4)), (1, 2, 8, 2.0))
    diag_inverse = gaussian(seeds[2], (SUPERS, W, W), 0.5, 4.0, ((2, 4),), jnp.float32)
    anc_tiles = draw_anc_tiles(jax.random.fold_in(seeds[5], 71), 0)
    slot_tile = draw_slot_tile(jax.random.fold_in(seeds[5], 71), 0)
    return {"resident_inverse": resident_inverse, "factor": factor, "diag_inverse": diag_inverse, "anc_tiles": anc_tiles, "slot_tile": slot_tile}


def slot_rows(anc_tiles, slot_tile):
    tile_ids = jnp.arange(NT, dtype=jnp.int32)
    listed = jnp.sum((anc_tiles[:, :, None] == tile_ids[None, None, :]).astype(jnp.float32), axis=1)
    onehot = (slot_tile[:, None] == tile_ids[None, :]).astype(jnp.float32)
    slot_mask = jnp.dot(listed, onehot.T, precision=lax.Precision.HIGHEST)
    return jnp.repeat(slot_mask, TB, axis=1)


def reference(resident_inverse, factor, diag_inverse, anc_tiles, slot_tile):
    row_mask = slot_rows(anc_tiles, slot_tile)
    masked = factor * row_mask.astype(jnp.bfloat16)[:, :, None]
    col_width = NA // N_COL

    def add_block(running, column_block):
        offset = column_block * col_width
        columns = lax.dynamic_slice_in_dim(resident_inverse, offset, col_width, 1).astype(jnp.float32)
        picked = lax.dynamic_slice_in_dim(masked, offset, col_width, 1).astype(jnp.float32)
        partial_value = jnp.einsum("rk,skw->srw", columns, picked, precision=lax.Precision.HIGHEST)
        rounded = lax.optimization_barrier(partial_value.astype(jnp.bfloat16))
        return running + rounded.astype(jnp.float32), None

    summed, _ = lax.scan(add_block, jnp.zeros((SUPERS, NA, W), jnp.float32), jnp.arange(N_COL, dtype=jnp.int32))
    new_cols = (-(summed * row_mask[:, :, None])).astype(jnp.bfloat16)
    diag_blocks = diag_inverse + jnp.einsum("snw,snv->swv", masked.astype(jnp.float32), summed, precision=lax.Precision.HIGHEST)
    return new_cols, diag_blocks
```

```python
import jax
import jax.numpy as jnp
from jax import lax
from jax.sharding import PartitionSpec as P


def slot_rows(anc_tiles, slot_tile, tile_rows):
    listed = (anc_tiles[:, :, None] == slot_tile[None, None, :]).any(axis=1)
    return jnp.repeat(listed.astype(jnp.float32), tile_rows, axis=1)


def on_device(resident_inverse, factor, diag_inverse, anc_tiles, slot_tile):
    own_rows = resident_inverse.shape[0]
    supers, _, part_width = factor.shape
    row_index = lax.axis_index("row")
    col_count = lax.axis_size("col")
    row_count = lax.axis_size("row")
    ratio = row_count // col_count
    total_rows = own_rows * row_count
    row_mask = slot_rows(anc_tiles, slot_tile, total_rows // slot_tile.shape[0])
    own_mask = lax.dynamic_slice_in_dim(row_mask, row_index * own_rows, own_rows, 1)
    mine = factor * own_mask.astype(jnp.bfloat16)[:, :, None]
    chunk = own_rows // row_count
    spread = mine.reshape(supers, row_count, chunk, part_width).transpose(1, 0, 2, 3)
    spread = lax.all_to_all(spread, "row", 0, 0, tiled=True)
    spread = spread.reshape(col_count, ratio * supers * chunk, part_width)
    spread = lax.all_to_all(spread, "col", 0, 0, tiled=True)
    spread = spread.reshape(col_count, ratio, supers, chunk, part_width)
    spread = spread.transpose(2, 1, 3, 0, 4).reshape(supers, ratio, chunk, col_count * part_width)
    spread, later = lax.optimization_barrier((spread, mine))
    col_index = lax.axis_index("col")

    last = col_count - 1
    up_moves = [(i, i + 1) for i in range(last)]
    down_moves = [(i + 1, i) for i in range(last)]

    def up(value):
        return lax.ppermute(value, "col", up_moves)

    def down(value):
        return lax.ppermute(value, "col", down_moves)

    gathered = [lax.all_gather(spread[s], "row", axis=1, tiled=True) for s in range(supers)]
    ups, downs = [later], [later]
    for by in range(last):
        low, high = ups[-1], downs[-1]
        if 0 < by <= supers:
            gathered[by - 1], low, high = lax.optimization_barrier((gathered[by - 1], low, high))
        ups.append(up(low))
        downs.append(down(high))
    partials = []
    for s in range(supers):
        blocks = gathered[s].reshape(ratio * own_rows, col_count * part_width)
        partials.append(
            jnp.dot(resident_inverse, blocks, preferred_element_type=jnp.float32).astype(jnp.bfloat16)
        )

    def piece(s, to):
        to = jnp.clip(to, 0, last) * part_width
        return lax.dynamic_slice_in_dim(partials[s], to, part_width, 1)

    kept = [piece(s, col_index) for s in range(supers)]
    kept[-1], ups, downs = lax.optimization_barrier((kept[-1], ups, downs))
    others = [later] + [ups[by] + downs[col_count - by] for by in range(1, col_count)]
    news, contribs = [], []
    for s in range(supers):
        from_below = piece(s, col_index + last)
        from_above = piece(s, col_index - last)
        for by in range(last, 0, -1):
            from_below, from_above = up(from_below), down(from_above)
            if by > 1:
                from_below = from_below + piece(s, col_index + by - 1)
                from_above = from_above + piece(s, col_index - by + 1)
        summed = (
            kept[s].astype(jnp.float32)
            + from_below.astype(jnp.float32)
            + from_above.astype(jnp.float32)
        )
        news.append((-(summed * own_mask[s][:, None])).astype(jnp.bfloat16))
        summed = summed.astype(jnp.bfloat16)
        contribs.append(jnp.stack([
            jnp.einsum("rw,rv->wv", other[s], summed, preferred_element_type=jnp.float32)
            for other in others
        ]))
    stacked = jnp.stack(contribs, axis=1)
    ordered = jnp.stack([
        lax.dynamic_index_in_dim(stacked, (col_index - q) % col_count, 0, keepdims=False)
        for q in range(col_count)
    ], axis=1)
    totals = ordered.reshape(supers, col_count * part_width, part_width)
    step = 1
    while step < row_count:
        sent = totals.astype(jnp.bfloat16)
        got = lax.ppermute(sent, "row", [(i, i ^ step) for i in range(row_count)])
        totals = sent.astype(jnp.float32) + got.astype(jnp.float32)
        step *= 2
    return (jnp.stack(news), diag_inverse + totals)


def solution(mesh):
    placed = (P("row", "col"), P(None, "row", "col"), P(None, None, "col"), P(), P())
    return jax.shard_map(
        on_device,
        mesh=mesh,
        in_specs=placed,
        out_specs=(P(None, "row", "col"), P(None, None, "col")),
        check_vma=False,
    )
```
